256 devices in a mesh: gx: 2 (over core), gy: 4 (over x), gz: 32 (over z, y).
Axes of the slice: x: 4, y: 4, z: 8, core: 2. Of those that a mesh axis runs over, the one named last changes fastest.
Arguments:
- resid_x: float32 [6, 8, 32, 120, 512], P('gx', 'gy', 'gz'), may hold values from -6 to 6
- resid_y: float32 [4, 12, 32, 120, 512], P('gx', 'gy', 'gz'), may hold values from -6 to 6
- face_weights: float32 [4, 8, 32, 4, 120], P('gx', 'gy', 'gz'), may hold values from 0.25 to 0.75
- face_counts: int32 [4, 8, 32, 4], P('gx', 'gy', 'gz'), may hold values from 1 to 4, as said below
- neumann: bfloat16 [4, 8, 32, 480, 480], P('gx', 'gy', 'gz'), may hold values from -0.25 to 0.25
- schur: bfloat16 [4, 8, 32, 480, 480], P('gx', 'gy', 'gz'), may hold values from -0.25 to 0.25
- basis: bfloat16 [4, 8, 32, 480, 64], P('gx', 'gy', 'gz'), may hold values from -0.25 to 0.25
- coarse_map: int32 [4, 8, 32, 64], P('gx', 'gy', 'gz'), may hold values from 0 to 511
- column_inverse: float32 [2, 4, 512, 512], P('gx', 'gy', 'gz'), may hold values from -0.25 to 0.25
- column_basis: float32 [2, 4, 512, 512], P('gx', 'gy', 'gz'), may hold values from -0.25 to 0.25
- top_inverse: float32 [512, 512], replicated, may hold values from -0.09375 to 0.09375
Outputs:
- z_x: float32 [6, 8, 32, 120, 512], P('gx', 'gy', 'gz')
- z_y: float32 [4, 12, 32, 120, 512], P('gx', 'gy', 'gz')
- schur_image: bfloat16 [4, 8, 32, 480, 512], P('gx', 'gy', 'gz')
The draws below stay inside these ranges and needn't reach their ends.
Inputs may be any that keep to these rules, and one draw needn't show every extreme that they name: `face_counts`: only the first 30 * count of a face's 120 dofs are live; about one face in eight has 4 live mesh faces. `coarse_map`: several local coarse dofs may share a column coarse dof.
All inputs are finite; a program needn't handle non-finite values.
Results may differ from the reference program's by a relative error of at most 0.0063.
Values sent between devices are 32-bit elements; how exact they have to be, the bound alone decides.
No kernel may reach another device: no remote copies, remote signals or barrier semaphores. Data moves between devices by JAX's collectives and lax.ppermute only.
A program may use at most 64 MiB of HBM per device.

```python
import jax
import jax.numpy as jnp
from jax import lax

BLK = 30
MAXB = 4
FW = 120
NI = 480
LOAD_CASES = 512
COARSE_DOFS = 64
NC2 = 512
NC3 = 512
N_GX = 2
N_GY = 4
N_GZ = 32


def draw_face_counts(key, part):
    picks = jax.random.randint(key, (2 * N_GX, 2 * N_GY, N_GZ, 4), 0, 8)
    values = jnp.where(picks == 0, MAXB, jnp.where(picks == 1, 2, 1))
    flat = values.reshape(-1).at[0].set(MAXB).at[1].set(1)
    return flat.reshape(2 * N_GX, 2 * N_GY, N_GZ, 4).astype(jnp.int32)


def place_ends(drawn, rng, least, high):
    shape = drawn.shape
    index_at = [jax.random.randint(jax.random.fold_in(rng, axis), (), 0, shape[axis]) for axis in range(len(shape))]
    drawn = drawn.at[tuple(index_at)].set(least)
    longest = shape.index(max(shape))
    index_at[longest] = (index_at[longest] + 1) % shape[longest]
    return drawn.at[tuple(index_at)].set(high)


def block_scale(own_key, shape, pieces, least, largest):
    def one(dim, shards_of):
        steps = jax.random.uniform(jax.random.fold_in(jax.random.fold_in(own_key, 6), dim), (shards_of,), jnp.float32, least / len(pieces), largest / len(pieces))
        return jnp.repeat(jnp.exp(steps), shape[dim] // shards_of).reshape((-1,) + (1,) * (len(shape) - dim - 1))

    level = one(*pieces[0])
    for cut in pieces[1:]:
        level = level * one(*cut)
    return level


def normal_values(stream_key, extent, width, limit, shards=(), kind=jnp.bfloat16):
    values = jax.random.normal(stream_key, extent, jnp.float32) * width
    if len(shards) > 0:
        values = block_scale(stream_key, extent, shards, -0.22, 0.18) * values
    return jnp.clip(values, min=-limit, max=limit).astype(kind)


def setup_inputs(seed: int = 0) -> dict:
    arg_keys = jax.random.split(jax.random.key(seed), 12)
    resid_x = normal_values(arg_keys[0], (3 * N_GX, 2 * N_GY, N_GZ, FW, LOAD_CASES), 1.0, 6.0, ((0, 2), (1, 4), (2, 32)), jnp.float32)
    resid_y = normal_values(arg_keys[1], (2 * N_GX, 3 * N_GY, N_GZ, FW, LOAD_CASES), 1.0, 6.0, ((0, 2), (1, 4), (2, 32)), jnp.float32)
    face_weights = jnp.clip(0.25 + 0.5 * jax.random.uniform(arg_keys[2], (2 * N_GX, 2 * N_GY, N_GZ, 4, FW), jnp.float32) ** block_scale(arg_keys[2], (2 * N_GX, 2 * N_GY, N_GZ, 4, FW), ((0, 2), (1, 4), (2, 32)), -0.2, 0.2), 0.25, 0.75)
    face_counts = draw_face_counts(jax.random.fold_in(arg_keys[11], 71), 0)
    neumann = normal_values(arg_keys[4], (2 * N_GX, 2 * N_GY, N_GZ, NI, NI), NI ** -0.5, 0.25, ((0, 2), (1, 4), (2, 32)))
    schur = normal_values(arg_keys[5], (2 * N_GX, 2 * N_GY, N_GZ, NI, NI), NI ** -0.5, 0.25, ((0, 2), (1, 4), (2, 32)))
    basis = normal_values(arg_keys[6], (2 * N_GX, 2 * N_GY, N_GZ, NI, COARSE_DOFS), NI ** -0.5, 0.25, ((0, 2), (1, 4), (2, 32)))
    coarse_map = place_ends(jax.random.randint(arg_keys[7], (2 * N_GX, 2 * N_GY, N_GZ, COARSE_DOFS), 0, NC2), jax.random.fold_in(arg_keys[7], 1), 0, NC2 - 1).astype(jnp.int32)
    column_inverse = normal_values(arg_keys[8], (N_GX, N_GY, NC2, NC2), NC2 ** -0.5, 0.25, ((0, 2), (1, 4), (2, 32)), jnp.float32)
    column_basis = normal_values(arg_keys[9], (N_GX, N_GY, NC2, NC3), NC2 ** -0.5, 0.25, ((0, 2), (1, 4), (2, 32)), jnp.float32)
    top_inverse = normal_values(arg_keys[10], (NC3, NC3), (NC3 * N_GX * N_GY) ** -0.5, 0.09375, (), jnp.float32)
    return {"resid_x": resid_x, "resid_y": resid_y, "face_weights": face_weights, "face_counts": face_counts, "neumann": neumann, "schur": schur, "basis": basis, "coarse_map": coarse_map, "column_inverse": column_inverse, "column_basis": column_basis, "top_inverse": top_inverse}


def physical_x(copies):
    rows = copies.reshape(N_GX, 3, 2 * N_GY, N_GZ, FW, LOAD_CASES)
    even = rows[:, 0] + jnp.roll(rows[:, 2], 1, axis=0)
    return jnp.stack([even, rows[:, 1]], 1).reshape(2 * N_GX, 2 * N_GY, N_GZ, FW, LOAD_CASES)


def physical_y(copies):
    rows = copies.reshape(2 * N_GX, N_GY, 3, N_GZ, FW, LOAD_CASES)
    even = rows[:, :, 0] + jnp.roll(rows[:, :, 2], 1, axis=1)
    return jnp.stack([even, rows[:, :, 1]], 2).reshape(2 * N_GX, 2 * N_GY, N_GZ, FW, LOAD_CASES)


def copies_x(faces):
    rows = faces.reshape(N_GX, 2, 2 * N_GY, N_GZ, FW, LOAD_CASES)
    stacked = jnp.stack([rows[:, 0], rows[:, 1], jnp.roll(rows[:, 0], -1, axis=0)], 1)
    return stacked.reshape(3 * N_GX, 2 * N_GY, N_GZ, FW, LOAD_CASES)


def copies_y(faces):
    rows = faces.reshape(2 * N_GX, N_GY, 2, N_GZ, FW, LOAD_CASES)
    stacked = jnp.stack([rows[:, :, 0], rows[:, :, 1], jnp.roll(rows[:, :, 0], -1, axis=1)], 2)
    return stacked.reshape(2 * N_GX, 3 * N_GY, N_GZ, FW, LOAD_CASES)


def sub_faces(face_x, face_y):
    return jnp.stack([face_x, jnp.roll(face_x, -1, axis=0), face_y, jnp.roll(face_y, -1, axis=1)], 3)


def to_columns(array):
    tail = array.shape[3:]
    moved = array.reshape((N_GX, 2, N_GY, 2, N_GZ) + tail).transpose((0, 2, 1, 3, 4) + tuple(range(5, 5 + len(tail))))
    return moved.reshape((N_GX, N_GY, 4 * N_GZ * tail[0]) + tail[1:])


def reference(resid_x, resid_y, face_weights, face_counts, neumann, schur, basis, coarse_map, column_inverse, column_basis, top_inverse):
    subdomain_count = 4 * N_GX * N_GY * N_GZ
    high = lax.Precision.HIGHEST
    dof_index = jnp.arange(FW, dtype=jnp.int32)
    live = (dof_index[None, None, None, None, :] < face_counts[..., None] * BLK).astype(jnp.float32)
    scale = face_weights * live
    faces = sub_faces(physical_x(resid_x), physical_y(resid_y))
    upart = (faces * scale[..., None]).reshape(subdomain_count, NI, LOAD_CASES).astype(jnp.bfloat16)
    nflat = neumann.reshape(subdomain_count, NI, NI)
    basis_flattened = basis.reshape(subdomain_count, NI, COARSE_DOFS)

    def first(items):
        vec, nmat, bmat = items
        wvec = jnp.dot(nmat, vec, preferred_element_type=jnp.float32)
        gvec = jnp.dot(bmat.T, vec, preferred_element_type=jnp.float32)
        return wvec, gvec

    weight_total, gall = lax.map(first, (upart, nflat, basis_flattened))
    gcol = to_columns(gall.reshape(2 * N_GX, 2 * N_GY, N_GZ, COARSE_DOFS, LOAD_CASES))
    mcol = to_columns(coarse_map.reshape(2 * N_GX, 2 * N_GY, N_GZ, COARSE_DOFS, 1))[..., 0]

    def scatter_one(target, values):
        return jnp.zeros((NC2, LOAD_CASES), jnp.float32).at[target].add(values)

    g2 = jax.vmap(jax.vmap(scatter_one))(mcol, gcol)
    y2 = jnp.einsum('abrk,abkn->abrn', column_inverse, g2, precision=high)
    g3 = jnp.einsum('abrk,abrn->kn', column_basis, g2, precision=high)
    y3 = jnp.dot(top_inverse, g3, precision=high)
    v2 = y2 + jnp.einsum('abrk,kn->abrn', column_basis, y3, precision=high)
    value_column = jnp.take_along_axis(v2, mcol[..., None], axis=2)
    subdomain_values = value_column.reshape(N_GX, N_GY, 2, 2, N_GZ, COARSE_DOFS, LOAD_CASES).transpose(0, 2, 1, 3, 4, 5, 6)
    subdomain_values = subdomain_values.reshape(subdomain_count, COARSE_DOFS, LOAD_CASES).astype(jnp.bfloat16)

    def second_level(items):
        wvec, bmat, coarse = items
        return wvec + jnp.dot(bmat, coarse, preferred_element_type=jnp.float32)

    output_total = lax.map(second_level, (weight_total, basis_flattened, subdomain_values))
    contrib = output_total.reshape(2 * N_GX, 2 * N_GY, N_GZ, 4, FW, LOAD_CASES) * scale[..., None]
    zphys_x = contrib[:, :, :, 0] + jnp.roll(contrib[:, :, :, 1], 1, axis=0)
    zphys_y = contrib[:, :, :, 2] + jnp.roll(contrib[:, :, :, 3], 1, axis=1)
    z_x = copies_x(zphys_x)
    z_y = copies_y(zphys_y)
    zsub = (sub_faces(zphys_x, zphys_y) * live[..., None]).reshape(subdomain_count, NI, LOAD_CASES).astype(jnp.bfloat16)

    def third(items):
        vec, smat = items
        return jnp.dot(smat, vec, preferred_element_type=jnp.float32).astype(jnp.bfloat16)

    image = lax.map(third, (zsub, schur.reshape(subdomain_count, NI, NI)))
    return z_x, z_y, image.reshape(2 * N_GX, 2 * N_GY, N_GZ, NI, LOAD_CASES)
```

```python
import functools

import jax
import jax.numpy as jnp
from jax import lax
from jax.experimental import pallas as pl
from jax.experimental.pallas import tpu as pltpu
from jax.sharding import Mesh, PartitionSpec as P

BLK = 30
YS = 4
LANES = 128
WIDE = 256
F32 = jnp.float32
BF16 = jnp.bfloat16
HIGH = lax.Precision.HIGHEST
NT = (((1,), (1,)), ((), ()))
TN = (((0,), (0,)), ((), ()))


def call(body, outs, *args, grid=None, ins=None, specs=None, scratch=(), mib=16):
    extra = {} if grid is None else {"grid": grid, "in_specs": ins, "out_specs": specs}
    return pl.pallas_call(
        body,
        out_shape=outs,
        scratch_shapes=scratch,
        compiler_params=pltpu.CompilerParams(vmem_limit_bytes=mib << 20),
        **extra,
    )(*args)


def shape(*dims, dtype=F32):
    return jax.ShapeDtypeStruct(dims, dtype)


def dot(a, b, dims=(((1,), (0,)), ((), ())), precision=None):
    return lax.dot_general(a, b, dims, precision=precision, preferred_element_type=F32)


def parts_of(value):
    first = value.astype(BF16)
    rest = value - first.astype(F32)
    second = rest.astype(BF16)
    third = (rest - second.astype(F32)).astype(BF16)
    return first, second, third


def live_columns(counts, dofs):
    index = lax.broadcasted_iota(jnp.int32, (dofs, 1), 0)
    out = []
    for s in range(4):
        for f in range(4):
            out.append((index < counts[s, f] * BLK).astype(F32))
    return out


def scale_columns(counts, weights, dofs):
    turned = weights[...].reshape(16, dofs).T
    live = live_columns(counts, dofs)
    return [turned[:, i : i + 1] * live[i] for i in range(16)], live


def face_list(x, y, i, j):
    return (x[i][j], x[i + 1][j], y[j][i], y[j + 1][i])


def front_body(counts, cmap, weights, basis, rx, ry, xb, xa, yb, ya, msg, u):
    dofs = rx.shape[3]
    scale, _ = scale_columns(counts, weights, dofs)
    x = [
        [rx[0, j, 0] + xb[j] for j in range(2)],
        [rx[1, j, 0] for j in range(2)],
        [rx[2, j, 0] + xa[j] for j in range(2)],
    ]
    y = [
        [ry[i, 0, 0] + yb[i] for i in range(2)],
        [ry[i, 1, 0] for i in range(2)],
        [ry[i, 2, 0] + ya[i] for i in range(2)],
    ]
    local = basis.shape[2]
    for s in range(4):
        i, j = divmod(s, 2)
        faces = face_list(x, y, i, j)
        part = jnp.concatenate([faces[f] * scale[4 * s + f] for f in range(4)], 0).astype(BF16)
        u[s] = part
        g = dot(basis[s], part, TN)
        for c in range(msg.shape[0]):
            msg[c, s * local : (s + 1) * local] = g[:, c * LANES : (c + 1) * LANES]
    tile = cmap[...].astype(F32)
    for c in range(msg.shape[0]):
        msg[c, 4 * local :] = tile


def inverse_body(mat, u, out):
    for s in range(mat.shape[0]):
        out[s] = dot(mat[s], u[s])


def scatter_body(msg, out, maps):
    local = 4 * 64
    size = out.shape[2]
    total = None
    index = lax.broadcasted_iota(jnp.int32, (size, LANES), 0)
    for c in range(YS):
        tile = msg[c, local:]
        maps[c] = tile
        hot = jnp.concatenate(
            [(index == tile[h : h + 1].astype(jnp.int32)).astype(F32).astype(BF16) for h in range(2)], 1
        )
        three = jnp.concatenate(parts_of(msg[c, :local]), 1)
        made = dot(hot, three)
        total = made if total is None else total + made
    total = total[:, :LANES] + total[:, LANES : 2 * LANES] + total[:, 2 * LANES :]
    out[...] = total.T.reshape(out.shape)


def fill(full, mats, which):
    zs, rows = mats.shape[1], mats.shape[3]
    for c in range(YS):
        for z in range(zs):
            full[(z * YS + c) * rows : (z * YS + c + 1) * rows] = mats[c, z, which]


def down_body(parts, mats, g2, g3, full):
    total = parts[0]
    for z in range(1, parts.shape[0]):
        total = total + parts[z]
    g2[...] = total
    fill(full, mats, 1)
    made = dot(total, full[...], precision=HIGH)
    for k in range(g3.shape[0]):
        g3[k] = made


def up_body(parts, g2, top, mats, out, inv, bas):
    total = parts[0]
    for z in range(1, parts.shape[0]):
        total = total + parts[z]
    fill(inv, mats, 0)
    fill(bas, mats, 1)
    y3 = dot(total, top[...], NT, precision=HIGH)
    v2 = dot(g2[...], inv[...], NT, precision=HIGH) + dot(y3, bas[...], NT, precision=HIGH)
    for k in range(out.shape[0]):
        out[k] = v2


def select_body(values, maps, out):
    zs, part, size = values.shape
    v2 = values[...].reshape(zs * part, size).astype(BF16)
    index = lax.broadcasted_iota(jnp.int32, (LANES, size), 1)
    for c in range(YS):
        turned = maps[c].astype(jnp.int32).T
        for h in range(2):
            hot = (index == turned[:, h : h + 1]).astype(F32).astype(BF16)
            out[c, h * LANES : (h + 1) * LANES] = dot(hot, v2, NT)


def contrib_body(counts, weights, basis, w, v, x0, x1, x2, y0, y1, y2):
    dofs = x0.shape[1]
    scale, _ = scale_columns(counts, weights, dofs)
    local = basis.shape[2]
    parts = []
    for s in range(4):
        vs = jnp.concatenate([v[c, s * local : (s + 1) * local] for c in range(v.shape[0])], 1)
        full = w[s] + dot(basis[s], vs.astype(BF16))
        parts.append([full[f * dofs : (f + 1) * dofs] * scale[4 * s + f] for f in range(4)])
    for j in range(2):
        x0[j] = parts[j][0]
        x1[j] = parts[j][1] + parts[2 + j][0]
        x2[j] = parts[2 + j][1]
    for i in range(2):
        y0[i] = parts[2 * i][2]
        y1[i] = parts[2 * i][3] + parts[2 * i + 1][2]
        y2[i] = parts[2 * i + 1][3]


def image_body(counts, schur, x0, x1, x2, y0, y1, y2, xb, xa, yb, ya, zx, zy, image):
    dofs = x0.shape[1]
    live = live_columns(counts, dofs)
    x = [
        [x0[j] + xb[j] for j in range(2)],
        [x1[j] for j in range(2)],
        [x2[j] + xa[j] for j in range(2)],
    ]
    y = [
        [y0[i] + yb[i] for i in range(2)],
        [y1[i] for i in range(2)],
        [y2[i] + ya[i] for i in range(2)],
    ]
    for k in range(3):
        for j in range(2):
            zx[k, j, 0] = x[k][j]
            zy[j, k, 0] = y[k][j]
    for s in range(4):
        i, j = divmod(s, 2)
        faces = face_list(x, y, i, j)
        z = jnp.concatenate([faces[f] * live[4 * s + f] for f in range(4)], 0).astype(BF16)
        image[s] = dot(schur[s], z).astype(BF16)


def swap(value, axis, step):
    size = lax.axis_size(axis)
    return lax.ppermute(value, axis, [(i, (i + step) % size) for i in range(size)])


def to_all(blocks, axes):
    return lax.all_to_all(blocks, axes, 0, 0, tiled=False)


def spread(value, axes):
    size = lax.axis_size(axes)
    return to_all(jnp.broadcast_to(value[None], (size,) + value.shape), axes)


def on_device(
    resid_x,
    resid_y,
    face_weights,
    face_counts,
    neumann,
    schur,
    basis,
    coarse_map,
    column_inverse,
    column_basis,
    top_inverse,
):
    dofs, loads = resid_x.shape[3:]
    inner = neumann.shape[3]
    local = basis.shape[4]
    size = column_inverse.shape[3]
    zs = lax.axis_size("z")
    rows = column_inverse.shape[2]
    xb = swap(resid_x[2, :, 0], "gx", 1)
    xa = swap(resid_x[0, :, 0], "gx", -1)
    yb = swap(resid_y[:, 2, 0], "gy", 1)
    ya = swap(resid_y[:, 0, 0], "gy", -1)

    mats = jnp.concatenate([column_inverse[0, 0], column_basis[0, 0]], 0)
    mats = spread(mats, "z").reshape(zs * 2 * rows, size)
    mats = spread(mats, "y").reshape(YS, zs, 2, rows, size)

    counts = face_counts.reshape(4, 4)
    weights = face_weights.reshape(4, 4, dofs)
    nmat = neumann.reshape(4, inner, inner)
    smat = schur.reshape(4, inner, inner)
    bmat = basis.reshape(4, inner, local)
    cmap = jnp.pad(coarse_map.reshape(2, LANES), ((0, 6), (0, 0)))

    smem = pl.BlockSpec(memory_space=pltpu.SMEM)
    steps = loads // WIDE

    def whole(a):
        return pl.BlockSpec(a.shape, lambda n, d=a.ndim: (0,) * d)

    def lanes(*lead):
        return pl.BlockSpec(lead + (WIDE,), lambda n, d=len(lead): (0,) * d + (n,))

    nmsg = WIDE // LANES
    msg_rows = 4 * local + 8
    face = lanes(2, dofs)
    msg, u = call(
        front_body,
        (shape(YS, msg_rows, LANES), shape(4, inner, loads, dtype=BF16)),
        counts, cmap, weights, bmat, resid_x, resid_y, xb, xa, yb, ya,
        grid=(steps,),
        ins=[smem, whole(cmap), whole(weights), whole(bmat), lanes(3, 2, 1, dofs), lanes(2, 3, 1, dofs)]
        + [face] * 4,
        specs=(pl.BlockSpec((nmsg, msg_rows, LANES), lambda n: (n, 0, 0)), lanes(4, inner)),
        mib=24,
    )
    w = call(
        inverse_body,
        shape(4, inner, loads),
        nmat, u,
        grid=(4,),
        ins=[
            pl.BlockSpec((1, inner, inner), lambda n: (n, 0, 0)),
            pl.BlockSpec((1, inner, loads), lambda n: (n, 0, 0)),
        ],
        specs=pl.BlockSpec((1, inner, loads), lambda n: (n, 0, 0)),
        mib=12,
    )
    got = to_all(msg, "y")
    block = loads // YS // zs
    g2p, maps = call(scatter_body, (shape(zs, block, size), shape(YS, 8, LANES)), got)
    got = to_all(g2p, "z")
    cols = lax.axis_size("gx") * lax.axis_size("gy")
    g2, g3 = call(
        down_body, (shape(block, size), shape(cols, block, size)), got, mats,
        scratch=[pltpu.VMEM((size, size), F32)],
    )
    got = to_all(g3, ("gx", "gy"))
    v2 = call(
        up_body, shape(zs, block, size), got, g2, top_inverse, mats,
        scratch=[pltpu.VMEM((size, size), F32)] * 2,
    )
    got = to_all(v2, "z")
    sel = call(select_body, shape(YS, 4 * local, LANES), got, maps)
    v = to_all(sel, "y")
    fshape = shape(2, dofs, loads)
    x0, x1, x2, y0, y1, y2 = call(
        contrib_body,
        (fshape,) * 6,
        counts, weights, bmat, w, v,
        grid=(steps,),
        ins=[smem, whole(weights), whole(bmat), lanes(4, inner),
             pl.BlockSpec((nmsg, 4 * local, LANES), lambda n: (n, 0, 0))],
        specs=(face,) * 6,
        mib=24,
    )
    xb = swap(x2, "gx", 1)
    xa = swap(x0, "gx", -1)
    yb = swap(y2, "gy", 1)
    ya = swap(y0, "gy", -1)
    z_x, z_y, image = call(
        image_body,
        (shape(3, 2, 1, dofs, loads), shape(2, 3, 1, dofs, loads), shape(4, inner, loads, dtype=BF16)),
        counts, smat, x0, x1, x2, y0, y1, y2, xb, xa, yb, ya,
        grid=(steps,),
        ins=[smem, whole(smat)] + [face] * 10,
        specs=(lanes(3, 2, 1, dofs), lanes(2, 3, 1, dofs), lanes(4, inner)),
        mib=32,
    )
    return z_x, z_y, image.reshape(2, 2, 1, inner, loads)


def solution(mesh):
    sizes = mesh.devices.shape
    split = Mesh(
        mesh.devices.reshape(sizes[0], sizes[1], sizes[2] // YS, YS), ("gx", "gy", "z", "y")
    )
    gz = ("z", "y")
    five = P("gx", "gy", gz, None, None)
    four = P("gx", "gy", gz, None)
    return jax.shard_map(
        on_device,
        mesh=split,
        in_specs=(five, five, five, four, five, five, five, four, four, four, P()),
        out_specs=(five, five, five),
        check_vma=False,
    )
```

```python
import jax
import jax.numpy as jnp
from jax import lax
from jax.experimental import pallas as pl
from jax.experimental.pallas import tpu as pltpu
from jax.sharding import Mesh, PartitionSpec as P


BLK = 30
YS = 4
LANES = 128
WIDE = 256
F32 = jnp.float32
BF16 = jnp.bfloat16
HIGH = lax.Precision.HIGHEST
NT = (((1,), (1,)), ((), ()))
TN = (((0,), (0,)), ((), ()))


def call(body, outs, *args, grid=None, ins=None, specs=None, scratch=(), mib=16):
    extra = {}
    if ins is not None:
        extra["in_specs"] = ins
    if grid is not None:
        extra.update(grid=grid, out_specs=specs)
    return pl.pallas_call(
        body,
        out_shape=outs,
        scratch_shapes=scratch,
        compiler_params=pltpu.CompilerParams(vmem_limit_bytes=mib << 20),
        **extra,
    )(*args)


def shape(*dims, dtype=F32):
    return jax.ShapeDtypeStruct(dims, dtype)


def dot(a, b, dims=(((1,), (0,)), ((), ())), precision=None):
    return lax.dot_general(a, b, dims, precision=precision, preferred_element_type=F32)


def parts_of(value):
    first = value.astype(BF16)
    rest = value - first.astype(F32)
    second = rest.astype(BF16)
    third = (rest - second.astype(F32)).astype(BF16)
    return first, second, third


def live_columns(counts, dofs):
    index = lax.broadcasted_iota(jnp.int32, (dofs, 1), 0)
    out = []
    for s in range(4):
        for f in range(4):
            out.append((index < counts[s, f] * BLK).astype(F32))
    return out


def scale_columns(counts, weights, dofs):
    turned = weights[...].reshape(16, dofs).T
    live = live_columns(counts, dofs)
    return [turned[:, i : i + 1] * live[i] for i in range(16)], live


def face_list(x, y, i, j):
    return (x[i][j], x[i + 1][j], y[j][i], y[j + 1][i])


def front_body(counts, cmap, weights, basis, rx, ry, xb, xa, yb, ya, msg, u):
    dofs = rx.shape[3]
    scale, _ = scale_columns(counts, weights, dofs)
    x = [
        [rx[0, j, 0] + xb[j] for j in range(2)],
        [rx[1, j, 0] for j in range(2)],
        [rx[2, j, 0] + xa[j] for j in range(2)],
    ]
    y = [
        [ry[i, 0, 0] + yb[i] for i in range(2)],
        [ry[i, 1, 0] for i in range(2)],
        [ry[i, 2, 0] + ya[i] for i in range(2)],
    ]
    local = basis.shape[2]
    for s in range(4):
        i, j = divmod(s, 2)
        faces = face_list(x, y, i, j)
        part = jnp.concatenate([faces[f] * scale[4 * s + f] for f in range(4)], 0).astype(BF16)
        u[s] = part
        g = dot(basis[s], part, TN)
        for c in range(msg.shape[0]):
            msg[c, (2 * j + i) * local : (2 * j + i + 1) * local] = g[:, c * LANES : (c + 1) * LANES]
    tile = cmap[...].astype(F32)
    for c in range(msg.shape[0]):
        msg[c, 4 * local :] = tile


def inverse_body(counts, weights, basis, mat, u, out, low, high):
    dofs, loads = low.shape[1], u.shape[2]
    local = basis.shape[2]
    s = pl.program_id(0)
    made = dot(mat[0], u[0])
    out[0] = made
    turned = weights[0].T
    index = lax.broadcasted_iota(jnp.int32, (dofs, 1), 0)

    def edge(ref, f):
        scale = turned[:, f : f + 1] * (index < counts[s, f] * BLK).astype(F32)
        ref[0, :, :loads] = made[f * dofs : (f + 1) * dofs] * scale
        ref[0, :, loads : loads + local] = basis[0, f * dofs : (f + 1) * dofs].astype(F32)
        ref[0, :, loads + local :] = jnp.broadcast_to(scale, (dofs, LANES - local))

    @pl.when(s % 2 == 0)
    def _():
        edge(low, 2)

    @pl.when(s % 2 == 1)
    def _():
        edge(high, 3)


def scatter_body(msg, out, maps):
    local = 4 * 64
    size = out.shape[2]
    total = None
    index = lax.broadcasted_iota(jnp.int32, (size, LANES), 0)
    for c in range(YS):
        tile = msg[c, local:]
        maps[c] = tile
        hot = jnp.concatenate(
            [(index == tile[h : h + 1].astype(jnp.int32)).astype(F32).astype(BF16) for h in range(2)], 1
        )
        three = jnp.concatenate(parts_of(msg[c, :local]), 1)
        made = dot(hot, three)
        total = made if total is None else total + made
    total = total[:, :LANES] + total[:, LANES : 2 * LANES] + total[:, 2 * LANES :]
    out[...] = total.T.reshape(out.shape)


def fill(full, place, mats, which):
    zs, rows = mats[0].shape[0], mats[0].shape[2]
    for k in range(YS):
        c = lax.rem(place[0] + YS - k, YS)
        for z in range(zs):
            start = pl.multiple_of((z * YS + c) * rows, rows)
            full[pl.ds(start, rows)] = mats[k][z, which]


def down_body(place, parts, m0, m1, m2, m3, g2, g3, full):
    total = parts[0]
    for z in range(1, parts.shape[0]):
        total = total + parts[z]
    g2[...] = total
    fill(full, place, (m0, m1, m2, m3), 1)
    made = dot(total, full[...], precision=HIGH)
    for k in range(g3.shape[0]):
        g3[k] = made


def level_body(place, g2, m0, m1, m2, m3, y2, full):
    fill(full, place, (m0, m1, m2, m3), 0)
    y2[...] = dot(g2[...], full[...], NT, precision=HIGH)


def up_body(place, parts, y2, top, m0, m1, m2, m3, out, full):
    total = parts[0]
    for z in range(1, parts.shape[0]):
        total = total + parts[z]
    fill(full, place, (m0, m1, m2, m3), 1)
    y3 = dot(total, top[...], NT, precision=HIGH)
    v2 = y2[...] + dot(y3, full[...], NT, precision=HIGH)
    for k in range(out.shape[0]):
        out[k] = v2


def select_body(values, maps, out):
    zs, part, size = values.shape
    v2 = values[...].reshape(zs * part, size).astype(BF16)
    index = lax.broadcasted_iota(jnp.int32, (LANES, size), 1)
    for c in range(YS):
        turned = maps[c].astype(jnp.int32).T
        for h in range(2):
            hot = (index == turned[:, h : h + 1]).astype(F32).astype(BF16)
            out[c, h * LANES : (h + 1) * LANES] = dot(hot, v2, NT)


def contrib_body(counts, weights, basis, w, v, x0, x1, x2, y0, y1, y2):
    dofs = x0.shape[1]
    scale, _ = scale_columns(counts, weights, dofs)
    local = basis.shape[2]
    parts = []
    for s in range(4):
        i, j = divmod(s, 2)
        q = (2 * j + i) * local
        vs = jnp.concatenate([v[c, q : q + local] for c in range(v.shape[0])], 1)
        full = w[s] + dot(basis[s], vs.astype(BF16))
        parts.append([full[f * dofs : (f + 1) * dofs] * scale[4 * s + f] for f in range(4)])
    for j in range(2):
        x0[j] = parts[j][0]
        x1[j] = parts[j][1] + parts[2 + j][0]
        x2[j] = parts[2 + j][1]
    for i in range(2):
        y0[i] = parts[2 * i][2]
        y1[i] = parts[2 * i][3] + parts[2 * i + 1][2]
        y2[i] = parts[2 * i + 1][3]


def beyond(edge, extra, v, i):
    local = v.shape[1] // 2
    vs = jnp.concatenate([v[c, i * local : (i + 1) * local] for c in range(v.shape[0])], 1)
    other = extra[i]
    return edge[i] + dot(other[:, :local].astype(BF16), vs.astype(BF16)) * other[:, local : local + 1]


def image_body(
    counts, schur, x0, x1, x2, y0, y1, y2, xb, xa, eb, ea, fb, fa, vb, va, zx, zy, image
):
    dofs = x0.shape[1]
    live = live_columns(counts, dofs)
    yb = [beyond(eb, fb, vb, i) for i in range(2)]
    ya = [beyond(ea, fa, va, i) for i in range(2)]
    x = [
        [x0[j] + xb[j] for j in range(2)],
        [x1[j] for j in range(2)],
        [x2[j] + xa[j] for j in range(2)],
    ]
    y = [
        [y0[i] + yb[i] for i in range(2)],
        [y1[i] for i in range(2)],
        [y2[i] + ya[i] for i in range(2)],
    ]
    for k in range(3):
        for j in range(2):
            zx[k, j, 0] = x[k][j]
            zy[j, k, 0] = y[k][j]
    for s in range(4):
        i, j = divmod(s, 2)
        faces = face_list(x, y, i, j)
        z = jnp.concatenate([faces[f] * live[4 * s + f] for f in range(4)], 0).astype(BF16)
        image[s] = dot(schur[s], z).astype(BF16)


def swap(value, axis, step):
    size = lax.axis_size(axis)
    return lax.ppermute(value, axis, [(i, (i + step) % size) for i in range(size)])


def to_all(blocks, axes):
    return lax.all_to_all(blocks, axes, 0, 0, tiled=False)


def spread(value, axes):
    size = lax.axis_size(axes)
    return to_all(jnp.broadcast_to(value[None], (size,) + value.shape), axes)


def on_device(
    resid_x,
    resid_y,
    face_weights,
    face_counts,
    neumann,
    schur,
    basis,
    coarse_map,
    column_inverse,
    column_basis,
    top_inverse,
):
    dofs, loads = resid_x.shape[3:]
    inner = neumann.shape[3]
    local = basis.shape[4]
    size = column_inverse.shape[3]
    zs = lax.axis_size("z")
    rows = column_inverse.shape[2]
    yb = swap(resid_y[:, 2, 0], "gy", 1)
    ya = swap(resid_y[:, 0, 0], "gy", -1)
    xb = swap(resid_x[2, :, 0], "gx", 1)
    xa = swap(resid_x[0, :, 0], "gx", -1)

    mats = jnp.concatenate([column_inverse[0, 0], column_basis[0, 0]], 0)
    mats = spread(mats, "z").reshape(zs, 2, rows, size)
    mats = [mats] + [swap(mats, "y", k) for k in range(1, YS)]
    place = lax.axis_index("y").reshape(1)

    counts = face_counts.reshape(4, 4)
    weights = face_weights.reshape(4, 4, dofs)
    nmat = neumann.reshape(4, inner, inner)
    smat = schur.reshape(4, inner, inner)
    bmat = basis.reshape(4, inner, local)
    cmap = coarse_map.reshape(2, 2, local).transpose(1, 0, 2).reshape(2, LANES)
    cmap = jnp.pad(cmap, ((0, 6), (0, 0)))

    smem = pl.BlockSpec(memory_space=pltpu.SMEM)
    vmem = pl.BlockSpec(memory_space=pltpu.VMEM)
    steps = loads // WIDE

    def whole(a):
        return pl.BlockSpec(a.shape, lambda n, d=a.ndim: (0,) * d)

    def lanes(*lead):
        return pl.BlockSpec(lead + (WIDE,), lambda n, d=len(lead): (0,) * d + (n,))

    def each(*tail):
        return pl.BlockSpec((1,) + tail, lambda n, d=len(tail): (n,) + (0,) * d)

    nmsg = WIDE // LANES
    msg_rows = 4 * local + 8
    face = lanes(2, dofs)
    msg, u = call(
        front_body,
        (shape(YS, msg_rows, LANES), shape(4, inner, loads, dtype=BF16)),
        counts, cmap, weights, bmat, resid_x, resid_y, xb, xa, yb, ya,
        grid=(steps,),
        ins=[smem, whole(cmap), whole(weights), whole(bmat), lanes(3, 2, 1, dofs), lanes(2, 3, 1, dofs)]
        + [face] * 4,
        specs=(pl.BlockSpec((nmsg, msg_rows, LANES), lambda n: (n, 0, 0)), lanes(4, inner)),
        mib=24,
    )
    pair = pl.BlockSpec((1, dofs, loads + LANES), lambda n: (n // 2, 0, 0))
    w, low, high = call(
        inverse_body,
        (shape(4, inner, loads),) + (shape(2, dofs, loads + LANES),) * 2,
        counts, weights, bmat, nmat, u,
        grid=(4,),
        ins=[smem, each(4, dofs), each(inner, local), each(inner, inner), each(inner, loads)],
        specs=(each(inner, loads), pair, pair),
        mib=16,
    )
    eb = swap(high, "gy", 1)
    ea = swap(low, "gy", -1)
    got = to_all(msg, "y")
    block = loads // YS // zs
    g2p, maps = call(scatter_body, (shape(zs, block, size), shape(YS, 8, LANES)), got)
    got = to_all(g2p, "z")
    cols = lax.axis_size("gx") * lax.axis_size("gy")
    full = [pltpu.VMEM((size, size), F32)]
    g2, g3 = call(
        down_body, (shape(block, size), shape(cols, block, size)), place, got, *mats,
        ins=[smem] + [vmem] * 5, scratch=full,
    )
    got = to_all(g3, ("gx", "gy"))
    y2 = call(
        level_body, shape(block, size), place, g2, *mats, ins=[smem] + [vmem] * 5, scratch=full
    )
    v2 = call(
        up_body, shape(zs, block, size), place, got, y2, top_inverse, *mats,
        ins=[smem] + [vmem] * 7, scratch=full,
    )
    got = to_all(v2, "z")
    sel = call(select_body, shape(YS, 4 * local, LANES), got, maps)
    v = to_all(sel, "y")
    vb = swap(v[:, 2 * local :], "gy", 1)
    va = swap(v[:, : 2 * local], "gy", -1)
    fshape = shape(2, dofs, loads)
    x0, x1, x2, y0, y1, y2 = call(
        contrib_body,
        (fshape,) * 6,
        counts, weights, bmat, w, v,
        grid=(steps,),
        ins=[smem, whole(weights), whole(bmat), lanes(4, inner),
             pl.BlockSpec((nmsg, 4 * local, LANES), lambda n: (n, 0, 0))],
        specs=(face,) * 6,
        mib=24,
    )
    xb = swap(x2, "gx", 1)
    xa = swap(x0, "gx", -1)
    extra = pl.BlockSpec((2, dofs, LANES), lambda n: (0, 0, loads // LANES))
    vspec = pl.BlockSpec((nmsg, 2 * local, LANES), lambda n: (n, 0, 0))
    z_x, z_y, image = call(
        image_body,
        (shape(3, 2, 1, dofs, loads), shape(2, 3, 1, dofs, loads), shape(4, inner, loads, dtype=BF16)),
        counts, smat, x0, x1, x2, y0, y1, y2, xb, xa, eb, ea, eb, ea, vb, va,
        grid=(steps,),
        ins=[smem, whole(smat)] + [face] * 10 + [extra] * 2 + [vspec] * 2,
        specs=(lanes(3, 2, 1, dofs), lanes(2, 3, 1, dofs), lanes(4, inner)),
        mib=32,
    )
    return z_x, z_y, image.reshape(2, 2, 1, inner, loads)


def solution(mesh):
    sizes = mesh.devices.shape
    split = Mesh(
        mesh.devices.reshape(sizes[0], sizes[1], sizes[2] // YS, YS), ("gx", "gy", "z", "y")
    )
    gz = ("z", "y")
    five = P("gx", "gy", gz, None, None)
    four = P("gx", "gy", gz, None)
    return jax.shard_map(
        on_device,
        mesh=split,
        in_specs=(five, five, five, four, five, five, five, four, four, four, P()),
        out_specs=(five, five, five),
        check_vma=False,
    )
```
